512 devices in a mesh: ctx: 64 (over y, x, core), tp: 8 (over z).
Axes of the slice: x: 4, y: 8, z: 8, core: 2. Of those that a mesh axis runs over, the one named last changes fastest.
Arguments:
- queries: bfloat16 [16384, 8192], P('ctx', 'tp'), may hold values from -6 to 6
- key_branch: bfloat16 [16384, 8192], P('ctx', 'tp'), may hold values from -6 to 6
- value_branch: bfloat16 [16384, 8192], P('ctx', 'tp'), may hold values from -6 to 6
- cotangent: bfloat16 [16384, 8192], P('ctx', 'tp'), may hold values from -6 to 6
- filters: float32 [512, 128], replicated, may hold values from -0.5 to 0.5
- skip_bias: float32 [8192], P('tp'), may hold values from -1 to 1
- contig_start: int32 [16384], replicated, may hold values from 0 to 16383, as said below
Outputs:
- output: bfloat16 [16384, 8192], P('ctx', 'tp')
- grad_query: bfloat16 [16384, 8192], P('ctx', 'tp')
- grad_key: bfloat16 [16384, 8192], P('ctx', 'tp')
- grad_value: bfloat16 [16384, 8192], P('ctx', 'tp')
- grad_filter: float32 [512, 128], replicated
- grad_bias: float32 [8192], P('tp')
The draws below stay inside these ranges and needn't reach their ends.
Inputs may be any that keep to these rules, and one draw needn't show every extreme that they name: contig_start[0] is 0, and for t > 0 contig_start[t] is either t (a new contig begins) or contig_start[t - 1]; the last token begins a contig of its own.
All inputs are finite; a program needn't handle non-finite values.
Results may differ from the reference program's by a relative error of at most 0.0056.
Values may be sent and summed in bfloat16 or wider, within the bound.
A program may use at most 64 MiB of HBM per device.

```python
import math
import jax
import jax.numpy as jnp
from jax import lax

D = 8192
FILT = 128
GROUPS = 512
TOKENS = 16384


def draw_contig_start(key, part):
    positions = jnp.arange(TOKENS, dtype=jnp.int32)
    marks = jax.random.randint(jax.random.fold_in(key, 17), (TOKENS,), 0, 256) == 0
    marks = jnp.where(positions == 0, True, marks)
    marks = jnp.where(positions == TOKENS - 1, True, marks)
    return lax.cummax(jnp.where(marks, positions, 0), axis=0)


def block_levels(key, extent, cuts, low, high):
    gain, own = 1.0, jax.random.fold_in(key, 6)
    for position, blocks in cuts:
        draws = jnp.exp(jax.random.uniform(jax.random.fold_in(own, position), (blocks,), jnp.float32, low / len(cuts), high / len(cuts)))
        gain = gain * jnp.repeat(draws, extent[position] // blocks).reshape([-1 if axis == position else 1 for axis in range(len(extent))])
    return gain


def noise(key, dims, scale, reach, shards=(), kind=jnp.bfloat16):
    values = scale * jax.random.normal(key, dims, jnp.float32)
    if shards:
        values = values * block_levels(key, dims, shards, -0.22, 0.18)
    return jnp.clip(values, -reach, reach).astype(kind)


def setup_inputs(seed: int = 0) -> dict:
    key_of = jax.random.split(jax.random.key(seed), 8)
    queries = noise(key_of[0], (TOKENS, D), 1.0, 6.0, ((0, 64), (1, 8)))
    key_branch = noise(key_of[1], (TOKENS, D), 1.0, 6.0, ((0, 64), (1, 8)))
    value_branch = noise(key_of[2], (TOKENS, D), 1.0, 6.0, ((0, 64), (1, 8)))
    cotangent = noise(key_of[3], (TOKENS, D), 1.0, 6.0, ((0, 64), (1, 8)))
    filters = noise(key_of[4], (GROUPS, FILT), FILT ** -0.5, 0.5, (), jnp.float32)
    skip_bias = jnp.clip(jax.random.uniform(key_of[5], (D,), jnp.float32, -1.0, 1.0) * block_levels(key_of[5], (D,), ((0, 8),), -0.4, 0.0), -1.0, 1.0)
    contig_start = draw_contig_start(jax.random.fold_in(key_of[7], 71), 0)
    return {"queries": queries, "key_branch": key_branch, "value_branch": value_branch, "cotangent": cotangent, "filters": filters, "skip_bias": skip_bias, "contig_start": contig_start}


def toeplitz(filter_taps):
    group_count, filter_size = filter_taps.shape
    leading = jnp.zeros((group_count, 1), filter_taps.dtype)
    trailing = jnp.zeros((group_count, filter_size), filter_taps.dtype)
    pattern = jnp.concatenate([leading, filter_taps[:, ::-1], trailing], axis=1)
    tiled = jnp.tile(pattern, (1, filter_size))[:, :2 * filter_size * filter_size]
    return tiled.reshape(group_count, filter_size, 2 * filter_size)

def fold_lags(products):
    filter_size, window_size = products.shape
    flattened = products.reshape(filter_size * window_size)
    flattened = jnp.concatenate([flattened, jnp.zeros((filter_size,), products.dtype)])
    columns = flattened.reshape(filter_size, window_size + 1).sum(axis=0)
    return columns[1:filter_size + 1][::-1]

def reference(queries, key_branch, value_branch, cotangent, filters, skip_bias, contig_start):
    token_count, channel_count = queries.shape
    group_count, filter_size = filters.shape
    per_group = channel_count // group_count
    block_count = token_count // filter_size
    gated_signal = (key_branch.astype(jnp.float32) * value_branch.astype(jnp.float32)).astype(jnp.bfloat16)
    signal_grad = (cotangent.astype(jnp.float32) * queries.astype(jnp.float32)).astype(jnp.bfloat16)
    filter_taps = lax.optimization_barrier(filters.astype(jnp.bfloat16)).astype(jnp.float32)
    band_all = toeplitz(filter_taps)
    row_starts = jnp.concatenate([contig_start.astype(jnp.int32), jnp.zeros((filter_size,), jnp.int32)])
    row_starts = row_starts.reshape(block_count + 1, filter_size)
    source_pos = (jnp.arange(block_count + 1, dtype=jnp.int32)[:, None] - 1) * filter_size
    source_pos = source_pos + jnp.arange(2 * filter_size, dtype=jnp.int32)[None, :]
    visible = source_pos[:, None, :] >= row_starts[:, :, None]

    def one_group(group):
        first_col = (group * per_group).astype(jnp.int32)

        def columns(array):
            return lax.dynamic_slice_in_dim(array, first_col, per_group, 1).astype(jnp.float32)
        query_part = columns(queries)
        key_part = columns(key_branch)
        value_part = columns(value_branch)
        cotangent_part = columns(cotangent)
        signal_part = columns(gated_signal)
        grad_part = columns(signal_grad)
        bias_part = lax.dynamic_slice_in_dim(skip_bias, first_col, per_group, 0).astype(jnp.float32)
        padded = jnp.concatenate([jnp.zeros((filter_size, per_group), jnp.float32), signal_part], axis=0)
        windows = jnp.concatenate([padded[:token_count].reshape(block_count, filter_size, per_group), padded[filter_size:].reshape(block_count, filter_size, per_group)], axis=1)
        grads_ext = jnp.concatenate([grad_part, jnp.zeros((filter_size, per_group), jnp.float32)], axis=0)
        grads_ext = grads_ext.reshape(block_count + 1, filter_size, per_group)
        band = jnp.where(visible, band_all[group][None], jnp.zeros((), jnp.float32))
        convolved = jnp.einsum('bts,bsc->btc', band[:block_count], windows).reshape(token_count, per_group)
        back_terms = jnp.einsum('bts,btc->bsc', band, grads_ext)
        gated_grad = (back_terms[:block_count, filter_size:] + back_terms[1:, :filter_size]).reshape(token_count, per_group)
        filtered = convolved + bias_part[None, :] * signal_part
        output = (query_part * filtered).astype(jnp.bfloat16)
        grad_query = (cotangent_part * filtered).astype(jnp.bfloat16)
        gated_grad = gated_grad + bias_part[None, :] * grad_part
        grad_key = (gated_grad * value_part).astype(jnp.bfloat16)
        grad_value = (gated_grad * key_part).astype(jnp.bfloat16)
        bias_term = lax.optimization_barrier(jnp.sum(grad_part * signal_part, axis=0))
        products = jnp.einsum('btc,bsc->bts', grads_ext[:block_count], windows)
        products = jnp.where(visible[:block_count], products, jnp.zeros((), jnp.float32)).sum(axis=0)
        return (output, grad_query, grad_key, grad_value, fold_lags(products), bias_term)
    pieces = lax.map(one_group, jnp.arange(group_count, dtype=jnp.int32))

    def merge_groups(stacked):
        return jnp.transpose(stacked, (1, 0, 2)).reshape(token_count, channel_count)
    filter_scale = 1.0 / math.sqrt(token_count * per_group)
    bias_scale = 1.0 / math.sqrt(token_count)
    grad_filter = pieces[4] * filter_scale
    grad_bias = pieces[5].reshape(channel_count) * bias_scale
    return (merge_groups(pieces[0]), merge_groups(pieces[1]), merge_groups(pieces[2]), merge_groups(pieces[3]), grad_filter, grad_bias)
```

```python
import functools
import math

import jax
import jax.numpy as jnp
from jax import lax
from jax.experimental import pallas as pl
from jax.experimental.pallas import tpu as pltpu
from jax.sharding import PartitionSpec as P

F32 = jnp.float32
BF16 = jnp.bfloat16
MESH = pl.DeviceIdType.MESH
ROW = 8
NT = (((1,), (1,)), ((), ()))


def iotas():
    down = lax.broadcasted_iota(jnp.int32, (128, 128), 0)
    across = lax.broadcasted_iota(jnp.int32, (128, 128), 1)
    return down, across


def conv_kernel(
    starts_ref, q_ref, k_ref, v_ref, c_ref, uh_ref, gh_ref, f_ref, b_ref,
    o_ref, gq_ref, gk_ref, gv_ref, gf_ref, gb_ref, pair_ref, lag_ref, ct_ref, bt_ref,
):
    s, t = iotas()

    @pl.when(pl.program_id(0) == 0)
    def _():
        start = [jnp.broadcast_to(starts_ref[i : i + 1, :], (128, 128)) for i in range(3)]
        lower = (s <= t).astype(F32)
        for b in range(3):
            pair_ref[2 * b] = ((1.0 - lower) * (s + 128 * (b - 1) >= start[b]).astype(F32)).astype(BF16)
            if b < 2:
                pair_ref[2 * b + 1] = (lower * (s + 128 * b >= start[b]).astype(F32)).astype(BF16)
                limit = jnp.where(127 - s <= t, start[b], start[b + 1])
                lag_ref[b] = (127 - s + 128 * b >= limit).astype(F32)

    q, k, v, c = (ref[...].astype(F32) for ref in (q_ref, k_ref, v_ref, c_ref))
    u = (k * v).astype(BF16)
    g = (c * q).astype(BF16)
    u_turned = jnp.concatenate([uh_ref[...], u], axis=0).T
    g_turned = jnp.concatenate([g, gh_ref[...]], axis=0).T
    gb_ref[...] = jnp.sum(u.astype(F32) * g.astype(F32), axis=0, keepdims=True)
    taps = f_ref[...].astype(BF16).astype(F32)
    flip = (s + t == 127).astype(F32).astype(BF16)
    flipped = [
        jnp.dot(flip, u[128 * i : 128 * i + 128], preferred_element_type=F32).astype(BF16)
        for i in range(2)
    ]
    upper = 127 - s <= t
    owner = lax.shift_right_logical(t, 4)
    none = jnp.zeros((128, 128), BF16)
    for i in range(8):
        rows = slice(16 * i, 16 * i + 16)
        ring = pltpu.roll(
            jnp.broadcast_to(taps[i : i + 1, :], (128, 128)), 0, 1, stride=1, stride_axis=0
        ).astype(BF16)
        p0, c0, p1, c1, p2 = (ring * pair_ref[n] for n in range(5))
        u_rows, g_rows = u_turned[rows], g_turned[rows]
        ct_ref[rows, 0:128] = jnp.dot(
            u_rows[:, 0:256], jnp.concatenate([p0, c0], 0), preferred_element_type=F32
        )
        ct_ref[rows, 128:256] = jnp.dot(
            u_rows[:, 128:384], jnp.concatenate([p1, c1], 0), preferred_element_type=F32
        )
        bt_ref[rows, 0:128] = lax.dot_general(
            g_rows[:, 0:256], jnp.concatenate([c0, p1], 1), NT, preferred_element_type=F32
        )
        bt_ref[rows, 128:256] = lax.dot_general(
            g_rows[:, 128:384], jnp.concatenate([c1, p2], 1), NT, preferred_element_type=F32
        )
        mine = owner == i
        first = jnp.dot(
            jnp.where(mine, flipped[0], none), g_turned[:, 0:256], preferred_element_type=F32
        )
        second = jnp.dot(
            jnp.where(mine, flipped[1], none), g_turned[:, 128:384], preferred_element_type=F32
        )
        lags = jnp.where(upper, first[:, :128], first[:, 128:]) * lag_ref[0]
        lags = lags + jnp.where(upper, second[:, :128], second[:, 128:]) * lag_ref[1]
        lags = pltpu.roll(lags, 1, 1, stride=1, stride_axis=0)
        gf_ref[i : i + 1, :] = jnp.sum(lags, axis=0, keepdims=True)
    bias = b_ref[...]
    filtered = ct_ref[...].T + bias * u.astype(F32)
    o_ref[...] = (q * filtered).astype(BF16)
    gq_ref[...] = (c * filtered).astype(BF16)
    gated_grad = bt_ref[...].T + bias * g.astype(F32)
    gk_ref[...] = (gated_grad * v).astype(BF16)
    gv_ref[...] = (gated_grad * k).astype(BF16)


def conv(starts, q, k, v, c, u_halo, g_halo, taps, bias):
    tokens, channels = q.shape
    tile = pl.BlockSpec((tokens, 128), lambda i: (0, i))
    halo = pl.BlockSpec((128, 128), lambda i: (0, i))
    line = pl.BlockSpec((1, 128), lambda i: (0, i))
    group = pl.BlockSpec((8, 128), lambda i: (i, 0))
    return pl.pallas_call(
        conv_kernel,
        grid=(channels // 128,),
        in_specs=[pl.BlockSpec((8, 128), lambda i: (0, 0))] + [tile] * 4 + [halo] * 2 + [group, line],
        out_specs=[tile] * 4 + [group, line],
        out_shape=[jax.ShapeDtypeStruct((tokens, channels), BF16)] * 4
        + [
            jax.ShapeDtypeStruct((channels // 16, 128), F32),
            jax.ShapeDtypeStruct((1, channels), F32),
        ],
        scratch_shapes=[
            pltpu.VMEM((5, 128, 128), BF16),
            pltpu.VMEM((2, 128, 128), F32),
            pltpu.VMEM((128, 256), F32),
            pltpu.VMEM((128, 256), F32),
        ],
    )(starts, q, k, v, c, u_halo, g_halo, taps, bias)


def reduce_kernel(
    part_ref, bias_ref, out_ref, bias_out_ref, row_in, col_in, bias_row, bias_col, total,
    row_s, row_r, col_s, col_r, brow_s, brow_r, bcol_s, bcol_r, z_s, z_r, x_s, x_r, c_s, c_r, out_sem,
):
    shard = lax.axis_index("ctx")
    z = lax.axis_index("tp")
    columns = lax.axis_size("ctx") // ROW
    layers = lax.axis_size("tp")
    place = lax.rem(shard, ROW)
    y = shard // ROW
    x, core = place // 2, lax.rem(place, 2)

    def along_row(step):
        to = lax.rem(place + step, ROW)
        return to, {"ctx": y * ROW + to, "tp": z}

    def along_y(step):
        to = lax.rem(y + step, columns)
        return to, {"ctx": to * ROW + place, "tp": z}

    def along_z(step):
        to = lax.rem(z + step, layers)
        return to, {"ctx": shard, "tp": to}

    def along_x(step):
        to = lax.rem(x + step, ROW // 2)
        return to, {"ctx": y * ROW + to * 2 + core, "tp": z}

    other = {"ctx": y * ROW + x * 2 + 1 - core, "tp": z}
    routes = [(along_row, ROW), (along_y, columns), (along_z, layers)]

    barrier = pltpu.get_barrier_semaphore()
    for route, size in routes:
        for step in range(1, size):
            pl.semaphore_signal(barrier, inc=1, device_id=route(step)[1], device_id_type=MESH)
    pl.semaphore_wait(barrier, sum(size - 1 for _, size in routes))

    def copy(source, target, send, receive, device):
        return pltpu.make_async_remote_copy(
            src_ref=source, dst_ref=target, send_sem=send, recv_sem=receive,
            device_id=device, device_id_type=MESH,
        )

    sent = []

    def send(*args):
        descriptor = copy(*args)
        descriptor.start()
        sent.append(descriptor)

    for step in range(1, ROW):
        to, device = along_row(step)
        send(part_ref.at[to], row_in.at[place], row_s.at[step], row_r.at[place], device)
        send(bias_ref, bias_row.at[place], brow_s.at[step], brow_r.at[place], device)
    row_in[place] = part_ref[place]
    bias_row[place] = bias_ref[...]
    for step in range(1, ROW):
        source, device = along_row(step)
        copy(part_ref.at[0], row_in.at[source], row_s.at[step], row_r.at[source], device).wait_recv()
        copy(bias_ref, bias_row.at[source], brow_s.at[step], brow_r.at[source], device).wait_recv()
    col_in[y] = jnp.sum(row_in[...], axis=0)
    bias_col[y] = jnp.sum(bias_row[...], axis=0)
    for step in range(1, columns):
        _, device = along_y(step)
        send(col_in.at[y], col_in.at[y], col_s.at[step], col_r.at[y], device)
        send(bias_col.at[y], bias_col.at[y], bcol_s.at[step], bcol_r.at[y], device)
    for step in range(1, columns):
        source, device = along_y(step)
        copy(col_in.at[y], col_in.at[source], col_s.at[step], col_r.at[source], device).wait_recv()
        copy(bias_col.at[y], bias_col.at[source], bcol_s.at[step], bcol_r.at[source], device).wait_recv()
    total[z, place] = jnp.sum(col_in[...], axis=0)
    bias_out_ref[...] = jnp.sum(bias_col[...], axis=0)
    for step in range(1, layers):
        _, device = along_z(step)
        send(total.at[z, place], total.at[z, place], z_s.at[step], z_r.at[z], device)
    for step in range(1, layers):
        source, device = along_z(step)
        copy(total.at[z, place], total.at[source, place], z_s.at[step], z_r.at[source], device).wait_recv()
    for step in range(1, ROW // 2):
        _, device = along_x(step)
        send(total.at[:, place], total.at[:, place], x_s.at[step], x_r.at[x], device)
    send(total.at[:, place], total.at[:, place], c_s.at[0], c_r.at[x], other)
    for step in range(1, ROW // 2):
        source, device = along_x(step)
        block = total.at[:, source * 2 + core]
        copy(block, block, x_s.at[step], x_r.at[source], device).wait_recv()
        send(block, block, c_s.at[step], c_r.at[source], other)
    for source in range(ROW // 2):
        block = total.at[:, source * 2 + 1 - core]
        copy(block, block, c_s.at[0], c_r.at[source], other).wait_recv()
    done = pltpu.make_async_copy(total, out_ref, out_sem)
    done.start()
    for descriptor in sent:
        descriptor.wait_send()
    done.wait()


def reduce(columns, layers, part, bias):
    dma = pltpu.SemaphoreType.DMA
    slice_shape = part.shape[1:]
    return pl.pallas_call(
        reduce_kernel,
        in_specs=[pl.BlockSpec(memory_space=pltpu.VMEM)] * 2,
        out_specs=[pl.BlockSpec(memory_space=pl.ANY), pl.BlockSpec(memory_space=pltpu.VMEM)],
        out_shape=[
            jax.ShapeDtypeStruct((layers, ROW, *slice_shape), F32),
            jax.ShapeDtypeStruct(bias.shape, F32),
        ],
        scratch_shapes=[
            pltpu.VMEM((ROW, *slice_shape), F32),
            pltpu.VMEM((columns, *slice_shape), F32),
            pltpu.VMEM((ROW, *bias.shape), F32),
            pltpu.VMEM((columns, *bias.shape), F32),
            pltpu.VMEM((layers, ROW, *slice_shape), F32),
            dma((ROW,)), dma((ROW,)), dma((columns,)), dma((columns,)),
            dma((ROW,)), dma((ROW,)), dma((columns,)), dma((columns,)),
            dma((layers,)), dma((layers,)), dma((ROW // 2,)), dma((ROW // 2,)),
            dma((ROW // 2,)), dma((ROW // 2,)), dma,
        ],
        compiler_params=pltpu.CompilerParams(collective_id=0, has_side_effects=True),
    )(part, bias)


def body(q, k, v, c, filters, bias, contig_start):
    tokens, channels = q.shape
    group_total, taps = filters.shape
    count, layers = lax.axis_size("ctx"), lax.axis_size("tp")
    shard, z = lax.axis_index("ctx"), lax.axis_index("tp")
    groups = group_total // layers
    token_count = tokens * count

    def gate(a, b):
        return (a.astype(F32) * b.astype(F32)).astype(BF16)

    u_edge = gate(k[-taps:], v[-taps:])
    g_edge = gate(c[:taps], q[:taps])
    u_halo = lax.ppermute(u_edge, "ctx", [(i, (i + 1) % count) for i in range(count)])
    g_halo = lax.ppermute(g_edge, "ctx", [(i, (i - 1) % count) for i in range(count)])
    far = jnp.full((6 * taps,), token_count, jnp.int32)
    starts = lax.dynamic_slice_in_dim(jnp.concatenate([contig_start, far]), shard * tokens, 8 * taps)
    starts = starts.reshape(8, taps) - shard * tokens
    mine = lax.dynamic_slice_in_dim(filters, z * groups, groups, 0)
    o, gq, gk, gv, part, bias_part = conv(
        starts, q, k, v, c, u_halo, g_halo, mine, bias.reshape(1, channels)
    )
    total, bias_total = reduce(
        count // ROW, layers, part.reshape(ROW, groups // ROW, taps), bias_part.reshape(8, channels // 8)
    )
    grad_filter = total.reshape(group_total, taps) * (1.0 / math.sqrt(token_count * (channels // groups)))
    grad_bias = bias_total.reshape(channels) * (1.0 / math.sqrt(token_count))
    return o, gq, gk, gv, grad_filter, grad_bias


def solution(mesh):
    return jax.shard_map(
        body,
        mesh=mesh,
        in_specs=(P("ctx", "tp"),) * 4 + (P(), P("tp"), P()),
        out_specs=(P("ctx", "tp"),) * 4 + (P(), P("tp")),
        check_vma=False,
    )
```

```python
import functools
import math

import jax
import jax.numpy as jnp
from jax import lax
from jax.experimental import pallas as pl
from jax.experimental.pallas import tpu as pltpu
from jax.sharding import PartitionSpec as P

F32 = jnp.float32
BF16 = jnp.bfloat16
MESH = pl.DeviceIdType.MESH
XS = 4
NT = (((1,), (1,)), ((), ()))


def iotas():
    down = lax.broadcasted_iota(jnp.int32, (128, 128), 0)
    across = lax.broadcasted_iota(jnp.int32, (128, 128), 1)
    return down, across


def dot(a, b):
    return jnp.dot(a, b, preferred_element_type=F32)


def whole_kernel(
    filter_scale, bias_scale,
    q_hbm, k_hbm, v_hbm, c_hbm, filters_hbm, skip_hbm, starts_hbm,
    o_ref, gq_ref, gk_ref, gv_ref, total, bias_total,
    q_ref, k_ref, v_ref, c_ref, taps_ref, skip_ref, starts_ref,
    u_edge, g_edge, u_halo, g_halo, u_turned, g_turned, u_flip,
    pair_ref, lag_ref, ct_ref, bt_ref,
    part, half_in, x_in, y_in, bias_part, bias_x, bias_y,
    in_sem, misc_sem, us, ur, gs, gr,
    c_s, c_r, x_s, x_r, y_s, y_r, bc_s, bc_r, bx_s, bx_r, by_s, by_r,
    z_s, z_r, gx_s, gx_r, gc_s, gc_r,
):
    shard, z = lax.axis_index("ctx"), lax.axis_index("tp")
    count, layers = lax.axis_size("ctx"), lax.axis_size("tp")
    columns = count // (2 * XS)
    tiles = q_ref.shape[0]
    groups = part.shape[0] * part.shape[1] * part.shape[2]
    y, x, core = shard // (2 * XS), lax.rem(shard, 2 * XS) // 2, lax.rem(shard, 2)

    def device(to_y, to_x, to_core, to_z):
        return {"ctx": (to_y * XS + to_x) * 2 + to_core, "tp": to_z}

    def along_x(step):
        to = lax.rem(x + step, XS)
        return to, device(y, to, core, z)

    def along_y(step):
        to = lax.rem(y + step, columns)
        return to, device(to, x, core, z)

    def along_z(step):
        to = lax.rem(z + step, layers)
        return to, device(y, x, core, to)

    other = device(y, x, 1 - core, z)
    right = {"ctx": lax.rem(shard + 1, count), "tp": z}
    left = {"ctx": lax.rem(shard + count - 1, count), "tp": z}

    def inputs(i):
        lanes = pl.ds(pl.multiple_of(i * 128, 128), 128)
        return [
            pltpu.make_async_copy(hbm.at[:, lanes], ref.at[i], in_sem.at[n, i])
            for n, (hbm, ref) in enumerate(
                ((q_hbm, q_ref), (k_hbm, k_ref), (v_hbm, v_ref), (c_hbm, c_ref))
            )
        ]

    small = [
        pltpu.make_async_copy(starts_hbm, starts_ref, misc_sem.at[0]),
        pltpu.make_async_copy(filters_hbm.at[pl.ds(pl.multiple_of(z * groups, 8), groups)], taps_ref, misc_sem.at[1]),
        pltpu.make_async_copy(skip_hbm, skip_ref, misc_sem.at[2]),
    ]

    barrier = pltpu.get_barrier_semaphore()
    friends = [left, right, other] + [along_x(step)[1] for step in range(1, XS)]
    friends += [along_y(step)[1] for step in range(1, columns)]
    friends += [along_z(step)[1] for step in range(1, layers)]
    for friend in friends:
        pl.semaphore_signal(barrier, inc=1, device_id=friend, device_id_type=MESH)

    @pl.loop(0, tiles)
    def _(i):
        for copy in inputs(i):
            copy.start()

    for copy in small:
        copy.start()

    s, t = iotas()
    flip = (s + t == 127).astype(F32).astype(BF16)

    def gates(i):
        q, k, v, c = (ref[i].astype(F32) for ref in (q_ref, k_ref, v_ref, c_ref))
        return q, k, v, c, (k * v).astype(BF16), (c * q).astype(BF16)

    @pl.loop(0, tiles)
    def _(i):
        for copy in inputs(i):
            copy.wait()
        u_edge[i] = (k_ref[i, 128:256].astype(F32) * v_ref[i, 128:256].astype(F32)).astype(BF16)
        g_edge[i] = (c_ref[i, 0:128].astype(F32) * q_ref[i, 0:128].astype(F32)).astype(BF16)

    pl.semaphore_wait(barrier, len(friends))
    sent = []

    def remote(source, target, send, receive, to):
        return pltpu.make_async_remote_copy(
            src_ref=source, dst_ref=target, send_sem=send, recv_sem=receive,
            device_id=to, device_id_type=MESH,
        )

    def u_copy(i):
        return remote(u_edge.at[i], u_halo.at[i], us.at[i], ur.at[i], right)

    def g_copy(i):
        return remote(g_edge.at[i], g_halo.at[i], gs.at[i], gr.at[i], left)

    def send(*args):
        descriptor = remote(*args)
        descriptor.start()
        sent.append(descriptor)

    @pl.loop(0, tiles)
    def _(i):
        g_copy(i).start()

    @pl.loop(0, tiles)
    def _(i):
        u_copy(i).start()

    @pl.loop(0, tiles, unroll=2)
    def _(i):
        q, k, v, c, u, g = gates(i)
        u_turned[i, :, 128:384] = u.T
        g_turned[i, :, 0:256] = g.T
        u_flip[i, 0:128] = dot(flip, u[0:128]).astype(BF16)
        u_flip[i, 128:256] = dot(flip, u[128:256]).astype(BF16)
        bias_part[pl.ds(i, 1)] = jnp.sum(u.astype(F32) * g.astype(F32), axis=0, keepdims=True)

    for copy in small:
        copy.wait()
    first_row = shard * 256
    rows = [starts_ref[pl.ds(jnp.minimum(2 * shard + b, 2 * count - 1), 1), :] - first_row for b in range(3)]
    rows[2] = rows[2] + jnp.where(shard == count - 1, 256 * count, 0)
    start = [jnp.broadcast_to(row, (128, 128)) for row in rows]
    lower = (s <= t).astype(F32)
    turned = 127 - s
    upper = (turned <= t).astype(F32)
    for b in range(3):
        pair_ref[2 * b] = ((1.0 - lower) * (s + 128 * (b - 1) >= start[b]).astype(F32)).astype(BF16)
        if b < 2:
            pair_ref[2 * b + 1] = (lower * (s + 128 * b >= start[b]).astype(F32)).astype(BF16)
            lag_ref[2 * b] = upper * (turned + 128 * b >= start[b]).astype(F32)
            lag_ref[2 * b + 1] = (1.0 - upper) * (turned + 128 * b >= start[b + 1]).astype(F32)

    owner = lax.shift_right_logical(t, 4)
    none = jnp.zeros((128, 128), BF16)
    above = turned <= t

    def fold(lags):
        lags = pltpu.roll(lags, 1, 1, stride=1, stride_axis=0)
        return jnp.sum(lags, axis=0, keepdims=True)

    def part_rows(i):
        return part.at[i // XS, lax.rem(i, XS)]

    def own_lags(i):
        mine_part = part_rows(i)
        for n in range(8):
            mine = owner == n
            first = dot(jnp.where(mine, u_flip[i, 0:128], none), g_turned[i, :, 0:256])
            second = dot(jnp.where(mine, u_flip[i, 128:256], none), g_turned[i, :, 128:256])
            lags = jnp.where(above, first[:, :128] , first[:, 128:]) * (lag_ref[0] + lag_ref[1])
            mine_part[n : n + 1, :] = fold(lags + second * lag_ref[2])

    def halo_lags(i):
        mine_part = part_rows(i)
        g_turned[i, :, 256:384] = g_halo[i].T
        for n in range(8):
            mine = owner == n
            far = dot(jnp.where(mine, u_flip[i, 128:256], none), g_turned[i, :, 256:384])
            mine_part[n : n + 1, :] += fold(far * lag_ref[3])

    send(bias_part, bias_x.at[0], bc_s, bc_r, other)

    @pl.loop(0, tiles, unroll=2)
    def _(i):
        own_lags(i)

    remote(bias_part, bias_x.at[0], bc_s, bc_r, other).wait_recv()
    bias_x[1 + x] = bias_part[...] + bias_x[0]
    for step in range(1, XS):
        _, to = along_x(step)
        send(bias_x.at[1 + x], bias_x.at[1 + x], bx_s.at[step], bx_r.at[x], to)

    @pl.loop(0, tiles, unroll=2)
    def _(i):
        g_copy(i).wait_recv()
        halo_lags(i)

    send(part.at[1 - core], half_in, c_s, c_r, other)

    @pl.loop(0, tiles)
    def _(i):
        u_copy(i).wait_recv()
        u_turned[i, :, 0:128] = u_halo[i].T

    for step in range(1, XS):
        source, to = along_x(step)
        remote(bias_x.at[1 + x], bias_x.at[1 + source], bx_s.at[step], bx_r.at[source], to).wait_recv()
    bias_y[y] = bias_x[1] + bias_x[2] + bias_x[3] + bias_x[4]
    for step in range(1, columns):
        _, to = along_y(step)
        send(bias_y.at[y], bias_y.at[y], by_s.at[step], by_r.at[y], to)

    def conv(i):
        q, k, v, c, u, g = gates(i)
        taps = taps_ref[pl.ds(pl.multiple_of(i * 8, 8), 8)].astype(BF16).astype(F32)
        for n in range(8):
            span = slice(16 * n, 16 * n + 16)
            ring = pltpu.roll(
                jnp.broadcast_to(taps[n : n + 1, :], (128, 128)), 0, 1, stride=1, stride_axis=0
            ).astype(BF16)
            p0, c0, p1, c1, p2 = (ring * pair_ref[m] for m in range(5))
            u_rows, g_rows = u_turned[i, span], g_turned[i, span]
            ct_ref[span, 0:128] = dot(u_rows[:, 0:256], jnp.concatenate([p0, c0], 0))
            ct_ref[span, 128:256] = dot(u_rows[:, 128:384], jnp.concatenate([p1, c1], 0))
            bt_ref[span, 0:128] = lax.dot_general(
                g_rows[:, 0:256], jnp.concatenate([c0, p1], 1), NT, preferred_element_type=F32
            )
            bt_ref[span, 128:256] = lax.dot_general(
                g_rows[:, 128:384], jnp.concatenate([c1, p2], 1), NT, preferred_element_type=F32
            )
        skip = skip_ref[pl.ds(i, 1)]
        filtered = ct_ref[...].T + skip * u.astype(F32)
        lanes = pl.ds(pl.multiple_of(i * 128, 128), 128)
        o_ref[:, lanes] = (q * filtered).astype(BF16)
        gq_ref[:, lanes] = (c * filtered).astype(BF16)
        gated_grad = bt_ref[...].T + skip * g.astype(F32)
        gk_ref[:, lanes] = (gated_grad * v).astype(BF16)
        gv_ref[:, lanes] = (gated_grad * k).astype(BF16)

    remote(part.at[1 - core], half_in, c_s, c_r, other).wait_recv()
    part[core] += half_in[...]
    for step in range(1, XS):
        to_x, to = along_x(step)
        send(part.at[core, to_x], x_in.at[x], x_s.at[step], x_r.at[x], to)
    x_in[x] = part[core, x]

    pl.loop(0, tiles // 2, unroll=2)(conv)

    for step in range(1, XS):
        source, to = along_x(step)
        remote(x_in.at[x], x_in.at[source], x_s.at[step], x_r.at[source], to).wait_recv()
    y_in[y] = x_in[0] + x_in[1] + x_in[2] + x_in[3]
    for step in range(1, columns):
        _, to = along_y(step)
        send(y_in.at[y], y_in.at[y], y_s.at[step], y_r.at[y], to)

    pl.loop(tiles // 2, tiles, unroll=2)(conv)

    for step in range(1, columns):
        source, to = along_y(step)
        remote(y_in.at[y], y_in.at[source], y_s.at[step], y_r.at[source], to).wait_recv()
    total[z, core, x] = jnp.sum(y_in[...], axis=0) * filter_scale
    for step in range(1, layers):
        _, to = along_z(step)
        send(total.at[z, core, x], total.at[z, core, x], z_s.at[step], z_r.at[z], to)

    for step in range(1, columns):
        source, to = along_y(step)
        remote(bias_y.at[y], bias_y.at[source], by_s.at[step], by_r.at[source], to).wait_recv()
    bias_total[...] = jnp.sum(bias_y[...], axis=0) * bias_scale

    for step in range(1, layers):
        source, to = along_z(step)
        remote(total.at[z, core, x], total.at[source, core, x], z_s.at[step], z_r.at[source], to).wait_recv()
    block = total.at[:, core, x]
    for step in range(1, XS):
        _, to = along_x(step)
        send(block, block, gx_s.at[step], gx_r.at[x], to)
    send(block, block, gc_s.at[x], gc_r.at[x], other)
    for step in range(1, XS):
        source, to = along_x(step)
        block = total.at[:, core, source]
        remote(block, block, gx_s.at[step], gx_r.at[source], to).wait_recv()
        send(block, block, gc_s.at[source], gc_r.at[source], other)

    @pl.loop(0, tiles)
    def _(i):
        u_copy(i).wait_send()
        g_copy(i).wait_send()

    for source in range(XS):
        block = total.at[:, 1 - core, source]
        remote(block, block, gc_s.at[source], gc_r.at[source], other).wait_recv()
    for descriptor in sent:
        descriptor.wait_send()


def whole(columns, layers, scales, q, k, v, c, filters, skip, starts):
    tokens, channels = q.shape
    tiles = channels // 128
    slice_shape = (channels // 16 // (2 * XS), 128)
    dma = pltpu.SemaphoreType.DMA
    anywhere = pl.BlockSpec(memory_space=pltpu.HBM)
    vmem = pltpu.VMEM
    block = vmem((tiles, tokens, 128), BF16)
    edge = vmem((tiles, 128, 128), BF16)
    return pl.pallas_call(
        functools.partial(whole_kernel, *scales),
        in_specs=[anywhere] * 7,
        out_specs=[pl.BlockSpec(memory_space=pltpu.VMEM)] * 6,
        out_shape=[jax.ShapeDtypeStruct((tokens, channels), BF16)] * 4
        + [
            jax.ShapeDtypeStruct((layers, 2, XS, *slice_shape), F32),
            jax.ShapeDtypeStruct((tiles, 128), F32),
        ],
        scratch_shapes=[block] * 4
        + [vmem((channels // 16, 128), F32), vmem((tiles, 128), F32), vmem(starts.shape, jnp.int32)]
        + [edge] * 4
        + [vmem((tiles, 128, 384), BF16)] * 2
        + [block]
        + [vmem((5, 128, 128), BF16), vmem((4, 128, 128), F32)]
        + [vmem((128, 256), F32)] * 2
        + [
            vmem((2, XS, *slice_shape), F32), vmem((XS, *slice_shape), F32),
            vmem((XS, *slice_shape), F32), vmem((columns, *slice_shape), F32),
            vmem((tiles, 128), F32), vmem((1 + XS, tiles, 128), F32),
            vmem((columns, tiles, 128), F32),
        ]
        + [dma((4, tiles)), dma((3,))]
        + [dma((tiles,))] * 4
        + [dma, dma, dma((XS,)), dma((XS,)), dma((columns,)), dma((columns,))]
        + [dma, dma, dma((XS,)), dma((XS,)), dma((columns,)), dma((columns,))]
        + [dma((layers,)), dma((layers,)), dma((XS,)), dma((XS,)), dma((XS,)), dma((XS,))],
        compiler_params=pltpu.CompilerParams(
            collective_id=0, has_side_effects=True, vmem_limit_bytes=20 * 2**20
        ),
    )(*(pltpu.with_memory_space_constraint(a, pltpu.HBM) for a in (q, k, v, c, filters, skip, starts)))


def deliver_kernel(count, *refs):
    sem = refs[-1]
    copies = [
        pltpu.make_async_copy(refs[n], refs[count + n], sem.at[n]) for n in range(count)
    ]
    for copy in copies:
        copy.start()
    for copy in copies:
        copy.wait()


def deliver(*arrays):
    return pl.pallas_call(
        functools.partial(deliver_kernel, len(arrays)),
        in_specs=[pl.BlockSpec(memory_space=pltpu.VMEM)] * len(arrays),
        out_specs=[pl.BlockSpec(memory_space=pl.ANY)] * len(arrays),
        out_shape=[jax.ShapeDtypeStruct(a.shape, a.dtype) for a in arrays],
        scratch_shapes=[pltpu.SemaphoreType.DMA((len(arrays),))],
        compiler_params=pltpu.CompilerParams(vmem_limit_bytes=20 * 2**20),
    )(*arrays)


def body(q, k, v, c, filters, skip, contig_start):
    tokens, channels = q.shape
    group_total, taps = filters.shape
    count, layers = lax.axis_size("ctx"), lax.axis_size("tp")
    token_count = tokens * count
    per_group = channels * layers // group_total
    scales = 1.0 / math.sqrt(token_count * per_group), 1.0 / math.sqrt(token_count)
    results = whole(
        count // (2 * XS), layers, scales, q, k, v, c, filters,
        skip.reshape(channels // 128, 128), contig_start.reshape(token_count // 128, 128),
    )
    o, gq, gk, gv, total, bias_total = deliver(*results)
    return o, gq, gk, gv, total.reshape(group_total, taps), bias_total.reshape(channels)


def solution(mesh):
    return jax.shard_map(
        body,
        mesh=mesh,
        in_specs=(P("ctx", "tp"),) * 4 + (P(), P("tp"), P()),
        out_specs=(P("ctx", "tp"),) * 4 + (P(), P("tp")),
        check_vma=False,
    )
```

```python
import functools
import math

import jax
import jax.numpy as jnp
from jax import lax
from jax.experimental import pallas as pl
from jax.experimental.pallas import tpu as pltpu
from jax.sharding import PartitionSpec as P

F32 = jnp.float32
BF16 = jnp.bfloat16
MESH = pl.DeviceIdType.MESH
XS = 4
NT = (((1,), (1,)), ((), ()))


def iotas():
    down = lax.broadcasted_iota(jnp.int32, (128, 128), 0)
    across = lax.broadcasted_iota(jnp.int32, (128, 128), 1)
    return down, across


def dot(a, b):
    return jnp.dot(a, b, preferred_element_type=F32)


def whole_kernel(
    filter_scale, bias_scale,
    q_hbm, k_hbm, v_hbm, c_hbm, filters_hbm, skip_hbm, starts_hbm,
    o_ref, gq_ref, gk_ref, gv_ref, total, bias_total,
    q_ref, k_ref, v_ref, c_ref, taps_ref, skip_ref, starts_ref,
    u_edge, g_edge, u_halo, g_halo, u_turned, g_turned, u_flip,
    pair_ref, lag_ref, ct_ref, bt_ref,
    acc, part, half_in, x_in, y_in, bias_part, bias_x, bias_y,
    in_sem, misc_sem, us, ur, gs, gr,
    c_s, c_r, x_s, x_r, y_s, y_r, bc_s, bc_r, bx_s, bx_r, by_s, by_r,
    z_s, z_r, gc_s, gc_r,
):
    shard, z = lax.axis_index("ctx"), lax.axis_index("tp")
    count, layers = lax.axis_size("ctx"), lax.axis_size("tp")
    columns = count // (2 * XS)
    tiles = q_ref.shape[0]
    groups = part.shape[0] * part.shape[1] * part.shape[2]
    y, x, core = shard // (2 * XS), lax.rem(shard, 2 * XS) // 2, lax.rem(shard, 2)

    def device(to_y, to_x, to_core, to_z):
        return {"ctx": (to_y * XS + to_x) * 2 + to_core, "tp": to_z}

    def along_x(step):
        to = lax.rem(x + step, XS)
        return to, device(y, to, core, z)

    def along_y(step):
        to = lax.rem(y + step, columns)
        return to, device(to, x, core, z)

    def along_z(step):
        to = lax.rem(z + step, layers)
        return to, device(y, x, core, to)

    other = device(y, x, 1 - core, z)
    right = {"ctx": lax.rem(shard + 1, count), "tp": z}
    left = {"ctx": lax.rem(shard + count - 1, count), "tp": z}

    def inputs(i):
        lanes = pl.ds(pl.multiple_of(i * 128, 128), 128)
        return [
            pltpu.make_async_copy(hbm.at[:, lanes], ref.at[i], in_sem.at[n, i])
            for n, (hbm, ref) in enumerate(
                ((q_hbm, q_ref), (k_hbm, k_ref), (v_hbm, v_ref), (c_hbm, c_ref))
            )
        ]

    small = [
        pltpu.make_async_copy(starts_hbm, starts_ref, misc_sem.at[0]),
        pltpu.make_async_copy(filters_hbm.at[pl.ds(pl.multiple_of(z * groups, 8), groups)], taps_ref, misc_sem.at[1]),
        pltpu.make_async_copy(skip_hbm, skip_ref, misc_sem.at[2]),
    ]

    barrier = pltpu.get_barrier_semaphore()
    friends = [left, right, other] + [along_x(step)[1] for step in range(1, XS)]
    friends += [along_y(step)[1] for step in range(1, columns)]
    friends += [along_z(step)[1] for step in range(1, layers)]
    def greet(some):
        for friend in some:
            pl.semaphore_signal(barrier, inc=1, device_id=friend, device_id_type=MESH)

    greet(friends[:2])

    @pl.loop(0, tiles)
    def _(i):
        for copy in inputs(i):
            copy.start()

    for copy in small:
        copy.start()
    greet(friends[2:])

    s, t = iotas()
    flip = (s + t == 127).astype(F32).astype(BF16)

    def gates(i):
        q, k, v, c = (ref[i].astype(F32) for ref in (q_ref, k_ref, v_ref, c_ref))
        return q, k, v, c, (k * v).astype(BF16), (c * q).astype(BF16)

    @pl.loop(0, tiles)
    def _(i):
        for copy in inputs(i):
            copy.wait()
        u_edge[i] = (k_ref[i, 128:256].astype(F32) * v_ref[i, 128:256].astype(F32)).astype(BF16)
        g_edge[i] = (c_ref[i, 0:128].astype(F32) * q_ref[i, 0:128].astype(F32)).astype(BF16)

    pl.semaphore_wait(barrier, len(friends))
    sent = []

    def remote(source, target, send, receive, to):
        return pltpu.make_async_remote_copy(
            src_ref=source, dst_ref=target, send_sem=send, recv_sem=receive,
            device_id=to, device_id_type=MESH,
        )

    def u_copy(i):
        return remote(u_edge.at[i], u_halo.at[i], us.at[i], ur.at[i], right)

    def g_copy(i):
        return remote(g_edge.at[i], g_halo.at[i], gs.at[i], gr.at[i], left)

    def send(*args):
        descriptor = remote(*args)
        descriptor.start()
        sent.append(descriptor)

    @pl.loop(0, tiles)
    def _(i):
        g_copy(i).start()

    @pl.loop(0, tiles)
    def _(i):
        u_copy(i).start()

    @pl.loop(0, tiles, unroll=2)
    def _(i):
        q, k, v, c, u, g = gates(i)
        u_turned[i, :, 128:384] = u.T
        g_turned[i, :, 0:256] = g.T
        u_flip[i, 0:128] = dot(flip, u[0:128]).astype(BF16)
        u_flip[i, 128:256] = dot(flip, u[128:256]).astype(BF16)
        bias_part[pl.ds(i, 1)] = jnp.sum(u.astype(F32) * g.astype(F32), axis=0, keepdims=True)

    for copy in small:
        copy.wait()
    first_row = shard * 256
    rows = [starts_ref[pl.ds(jnp.minimum(2 * shard + b, 2 * count - 1), 1), :] - first_row for b in range(3)]
    rows[2] = rows[2] + jnp.where(shard == count - 1, 256 * count, 0)
    start = [jnp.broadcast_to(row, (128, 128)) for row in rows]
    lower = (s <= t).astype(F32)
    turned = 127 - s
    above = turned <= t
    for b in range(3):
        pair_ref[2 * b] = ((1.0 - lower) * (s + 128 * (b - 1) >= start[b]).astype(F32)).astype(BF16)
        if b < 2:
            pair_ref[2 * b + 1] = (lower * (s + 128 * b >= start[b]).astype(F32)).astype(BF16)
            limit = jnp.where(above, start[b], start[b + 1])
            lag_ref[b] = (turned + 128 * b >= limit).astype(F32)

    owner = lax.shift_right_logical(t, 4)
    none = jnp.zeros((128, 128), BF16)

    def fold(lags):
        lags = pltpu.roll(lags, 1, 1, stride=1, stride_axis=0)
        return jnp.sum(lags, axis=0, keepdims=True)

    def part_rows(i):
        return part.at[i // XS, lax.rem(i, XS)]

    def lags(i, n, b):
        mine = jnp.where(owner == n, u_flip[i, 128 * b : 128 * b + 128], none)
        products = dot(mine, g_turned[i, :, 128 * b : 128 * b + 256])
        return jnp.where(above, products[:, :128], products[:, 128:]) * lag_ref[b]

    def own_lags(i):
        for n in range(8):
            acc[i, n] = lags(i, n, 0)

    def halo_lags(i):
        for n in range(8):
            both = pltpu.roll(acc[i, n] + lags(i, n, 1), 1, 1, stride=1, stride_axis=0)
            part[i // XS, lax.rem(i, XS), n : n + 1] = jnp.sum(both, axis=0, keepdims=True)

    send(bias_part, bias_x.at[0], bc_s, bc_r, other)

    @pl.loop(0, tiles, unroll=2)
    def _(i):
        own_lags(i)

    remote(bias_part, bias_x.at[0], bc_s, bc_r, other).wait_recv()
    bias_x[1 + x] = bias_part[...] + bias_x[0]
    for step in range(1, XS):
        _, to = along_x(step)
        send(bias_x.at[1 + x], bias_x.at[1 + x], bx_s.at[step], bx_r.at[x], to)

    @pl.loop(0, tiles // 2)
    def _(j):
        for i in range(2):
            g_copy(2 * j + i).wait_recv()
        for i in range(2):
            g_turned[2 * j + i, :, 256:384] = g_halo[2 * j + i].T
        for i in range(2):
            halo_lags(2 * j + i)

    send(part.at[1 - core], half_in, c_s, c_r, other)

    @pl.loop(0, tiles)
    def _(i):
        u_copy(i).wait_recv()
        u_turned[i, :, 0:128] = u_halo[i].T

    for step in range(1, XS):
        source, to = along_x(step)
        remote(bias_x.at[1 + x], bias_x.at[1 + source], bx_s.at[step], bx_r.at[source], to).wait_recv()
    bias_y[y] = bias_x[1] + bias_x[2] + bias_x[3] + bias_x[4]
    for step in range(1, columns):
        _, to = along_y(step)
        send(bias_y.at[y], bias_y.at[y], by_s.at[step], by_r.at[y], to)

    def conv(i):
        q, k, v, c, u, g = gates(i)
        taps = taps_ref[pl.ds(pl.multiple_of(i * 8, 8), 8)].astype(BF16).astype(F32)
        for n in range(8):
            span = slice(16 * n, 16 * n + 16)
            ring = pltpu.roll(
                jnp.broadcast_to(taps[n : n + 1, :], (128, 128)), 0, 1, stride=1, stride_axis=0
            ).astype(BF16)
            p0, c0, p1, c1, p2 = (ring * pair_ref[m] for m in range(5))
            u_rows, g_rows = u_turned[i, span], g_turned[i, span]
            ct_ref[span, 0:128] = dot(u_rows[:, 0:256], jnp.concatenate([p0, c0], 0))
            ct_ref[span, 128:256] = dot(u_rows[:, 128:384], jnp.concatenate([p1, c1], 0))
            bt_ref[span, 0:128] = lax.dot_general(
                g_rows[:, 0:256], jnp.concatenate([c0, p1], 1), NT, preferred_element_type=F32
            )
            bt_ref[span, 128:256] = lax.dot_general(
                g_rows[:, 128:384], jnp.concatenate([c1, p2], 1), NT, preferred_element_type=F32
            )
        skip = skip_ref[pl.ds(i, 1)]
        filtered = ct_ref[...].T + skip * u.astype(F32)
        lanes = pl.ds(pl.multiple_of(i * 128, 128), 128)
        o_ref[:, lanes] = (q * filtered).astype(BF16)
        gq_ref[:, lanes] = (c * filtered).astype(BF16)
        gated_grad = bt_ref[...].T + skip * g.astype(F32)
        gk_ref[:, lanes] = (gated_grad * v).astype(BF16)
        gv_ref[:, lanes] = (gated_grad * k).astype(BF16)

    remote(part.at[1 - core], half_in, c_s, c_r, other).wait_recv()
    part[core] += half_in[...]
    for step in range(1, XS):
        to_x, to = along_x(step)
        send(part.at[core, to_x], x_in.at[x], x_s.at[step], x_r.at[x], to)
    x_in[x] = part[core, x]

    pl.loop(0, tiles // 2)(conv)

    for step in range(1, XS):
        source, to = along_x(step)
        remote(x_in.at[x], x_in.at[source], x_s.at[step], x_r.at[source], to).wait_recv()
    y_in[y] = x_in[0] + x_in[1] + x_in[2] + x_in[3]
    for step in range(1, columns):
        _, to = along_y(step)
        send(y_in.at[y], y_in.at[y], y_s.at[step], y_r.at[y], to)

    pl.loop(tiles // 2, tiles)(conv)

    for step in range(1, columns):
        source, to = along_y(step)
        remote(y_in.at[y], y_in.at[source], y_s.at[step], y_r.at[source], to).wait_recv()
    total[z, core, x] = jnp.sum(y_in[...], axis=0) * filter_scale
    own = total.at[z, core, x]
    sheet = sorted(
        ((a, b) for a in range(layers) for b in range(XS) if a or b),
        key=lambda ab: -(min(ab[0], layers - ab[0]) + min(ab[1], XS - ab[1])),
    )
    for a, b in sheet:
        to = device(y, lax.rem(x + b, XS), core, lax.rem(z + a, layers))
        send(own, own, z_s.at[a, b], z_r.at[z, x], to)

    for step in range(1, columns):
        source, to = along_y(step)
        remote(bias_y.at[y], bias_y.at[source], by_s.at[step], by_r.at[source], to).wait_recv()
    bias_total[...] = jnp.sum(bias_y[...], axis=0) * bias_scale

    @pl.loop(0, tiles)
    def _(i):
        u_copy(i).wait_send()
        g_copy(i).wait_send()

    span = layers // 2
    for chunk in range(2):
        for a in range(chunk * span, chunk * span + span):
            for b in range(XS):
                @pl.when((a != z) | (b != x))
                def _():
                    there = total.at[a, core, b]
                    remote(there, there, z_s.at[0, 0], z_r.at[a, b], other).wait_recv()
        block = total.at[chunk * span : chunk * span + span, core]
        send(block, block, gc_s.at[chunk], gc_r.at[chunk], other)
    for chunk in range(2):
        block = total.at[chunk * span : chunk * span + span, 1 - core]
        remote(block, block, gc_s.at[chunk], gc_r.at[chunk], other).wait_recv()
    for descriptor in sent:
        descriptor.wait_send()


def whole(columns, layers, scales, q, k, v, c, filters, skip, starts):
    tokens, channels = q.shape
    tiles = channels // 128
    slice_shape = (channels // 16 // (2 * XS), 128)
    dma = pltpu.SemaphoreType.DMA
    anywhere = pl.BlockSpec(memory_space=pltpu.HBM)
    vmem = pltpu.VMEM
    block = vmem((tiles, tokens, 128), BF16)
    edge = vmem((tiles, 128, 128), BF16)
    return pl.pallas_call(
        functools.partial(whole_kernel, *scales),
        in_specs=[anywhere] * 7,
        out_specs=[pl.BlockSpec(memory_space=pltpu.VMEM)] * 6,
        out_shape=[jax.ShapeDtypeStruct((tokens, channels), BF16)] * 4
        + [
            jax.ShapeDtypeStruct((layers, 2, XS, *slice_shape), F32),
            jax.ShapeDtypeStruct((tiles, 128), F32),
        ],
        scratch_shapes=[block] * 4
        + [vmem((channels // 16, 128), F32), vmem((tiles, 128), F32), vmem(starts.shape, jnp.int32)]
        + [edge] * 4
        + [vmem((tiles, 128, 384), BF16)] * 2
        + [block]
        + [vmem((5, 128, 128), BF16), vmem((2, 128, 128), F32)]
        + [vmem((128, 256), F32)] * 2
        + [
            vmem((tiles, 8, 128, 128), F32),
            vmem((2, XS, *slice_shape), F32), vmem((XS, *slice_shape), F32),
            vmem((XS, *slice_shape), F32), vmem((columns, *slice_shape), F32),
            vmem((tiles, 128), F32), vmem((1 + XS, tiles, 128), F32),
            vmem((columns, tiles, 128), F32),
        ]
        + [dma((4, tiles)), dma((3,))]
        + [dma((tiles,))] * 4
        + [dma, dma, dma((XS,)), dma((XS,)), dma((columns,)), dma((columns,))]
        + [dma, dma, dma((XS,)), dma((XS,)), dma((columns,)), dma((columns,))]
        + [dma((layers, XS)), dma((layers, XS)), dma((2,)), dma((2,))],
        compiler_params=pltpu.CompilerParams(
            collective_id=0, has_side_effects=True, vmem_limit_bytes=24 * 2**20
        ),
    )(*(pltpu.with_memory_space_constraint(a, pltpu.HBM) for a in (q, k, v, c, filters, skip, starts)))


def deliver_kernel(count, *refs):
    sem = refs[-1]
    copies = [
        pltpu.make_async_copy(refs[n], refs[count + n], sem.at[n]) for n in range(count)
    ]
    for copy in copies:
        copy.start()
    for copy in copies:
        copy.wait()


def deliver(*arrays):
    return pl.pallas_call(
        functools.partial(deliver_kernel, len(arrays)),
        in_specs=[pl.BlockSpec(memory_space=pltpu.VMEM)] * len(arrays),
        out_specs=[pl.BlockSpec(memory_space=pl.ANY)] * len(arrays),
        out_shape=[jax.ShapeDtypeStruct(a.shape, a.dtype) for a in arrays],
        scratch_shapes=[pltpu.SemaphoreType.DMA((len(arrays),))],
        compiler_params=pltpu.CompilerParams(vmem_limit_bytes=20 * 2**20),
    )(*arrays)


def body(q, k, v, c, filters, skip, contig_start):
    tokens, channels = q.shape
    group_total, taps = filters.shape
    count, layers = lax.axis_size("ctx"), lax.axis_size("tp")
    token_count = tokens * count
    per_group = channels * layers // group_total
    scales = 1.0 / math.sqrt(token_count * per_group), 1.0 / math.sqrt(token_count)
    results = whole(
        count // (2 * XS), layers, scales, q, k, v, c, filters,
        skip.reshape(channels // 128, 128), contig_start.reshape(token_count // 128, 128),
    )
    o, gq, gk, gv, total, bias_total = deliver(*results)
    return o, gq, gk, gv, total.reshape(group_total, taps), bias_total.reshape(channels)


def solution(mesh):
    return jax.shard_map(
        body,
        mesh=mesh,
        in_specs=(P("ctx", "tp"),) * 4 + (P(), P("tp"), P()),
        out_specs=(P("ctx", "tp"),) * 4 + (P(), P("tp")),
        check_vma=False,
    )
```

```python
import functools
import math

import jax
import jax.numpy as jnp
from jax import lax
from jax.experimental import pallas as pl
from jax.experimental.pallas import tpu as pltpu
from jax.sharding import PartitionSpec as P

F32 = jnp.float32
BF16 = jnp.bfloat16
MESH = pl.DeviceIdType.MESH
XS = 4
NT = (((1,), (1,)), ((), ()))


def iotas():
    down = lax.broadcasted_iota(jnp.int32, (128, 128), 0)
    across = lax.broadcasted_iota(jnp.int32, (128, 128), 1)
    return down, across


def dot(a, b):
    return jnp.dot(a, b, preferred_element_type=F32)


def near(size):
    return sorted({1, 2, size - 2, size - 1} & set(range(1, size)))


def beyond(size):
    return [2, size - 2] if size > 5 else []


def whole_kernel(
    filter_scale, bias_scale,
    q_hbm, k_hbm, v_hbm, c_hbm, filters_hbm, skip_hbm, starts_hbm,
    o_ref, gq_ref, gk_ref, gv_ref, total, bias_total,
    q_ref, k_ref, v_ref, c_ref, taps_ref, skip_ref, starts_ref,
    u_edge, g_edge, u_halo, g_halo, u_turned, g_turned, u_flip,
    pair_ref, lag_ref, ct_ref, bt_ref,
    acc, part, half_in, x_in, y_in, bias_part, bias_x, bias_y,
    in_sem, misc_sem, us, ur, gs, gr,
    c_s, c_r, x_s, x_r, y_s, y_r, bc_s, bc_r, bx_s, bx_r, by_s, by_r,
    z_s, z_r, gc_s, gc_r, ready_sem,
):
    shard, z = lax.axis_index("ctx"), lax.axis_index("tp")
    count, layers = lax.axis_size("ctx"), lax.axis_size("tp")
    columns = count // (2 * XS)
    tiles = q_ref.shape[1] // 128
    groups = part.shape[0] * part.shape[1] * part.shape[2]
    y, x, core = shard // (2 * XS), lax.rem(shard, 2 * XS) // 2, lax.rem(shard, 2)

    def device(to_y, to_x, to_core, to_z):
        return {"ctx": (to_y * XS + to_x) * 2 + to_core, "tp": to_z}

    def far_first(size):
        return sorted(range(1, size), key=lambda step: -min(step, size - step))

    def along_x(step):
        to = lax.rem(x + step, XS)
        return to, device(y, to, core, z)

    def along_y(step):
        to = lax.rem(y + step, columns)
        return to, device(to, x, core, z)

    def along_z(step):
        to = lax.rem(z + step, layers)
        return to, device(y, x, core, to)

    other = device(y, x, 1 - core, z)
    right = {"ctx": lax.rem(shard + 1, count), "tp": z}
    left = {"ctx": lax.rem(shard + count - 1, count), "tp": z}

    def lanes_of(i):
        return pl.ds(pl.multiple_of(i * 128, 128), 128)

    low, high = pl.ds(0, 128), pl.ds(128, 128)
    sources = ((q_hbm, q_ref), (c_hbm, c_ref), (k_hbm, k_ref), (v_hbm, v_ref))
    edges, inner = (
        [
            pltpu.make_async_copy(hbm.at[rows], ref.at[rows], in_sem.at[base + n])
            for n, ((hbm, ref), rows) in enumerate(zip(sources, order))
        ]
        for base, order in ((0, (low, low, high, high)), (4, (high, high, low, low)))
    )

    small = [
        pltpu.make_async_copy(starts_hbm, starts_ref, misc_sem.at[0]),
        pltpu.make_async_copy(filters_hbm.at[pl.ds(pl.multiple_of(z * groups, 8), groups)], taps_ref, misc_sem.at[1]),
        pltpu.make_async_copy(skip_hbm, skip_ref, misc_sem.at[2]),
    ]

    barrier = pltpu.get_barrier_semaphore()
    friends = [left, right, other] + [along_x(step)[1] for step in range(1, XS)]
    friends += [along_y(step)[1] for step in near(columns)]
    friends += [along_z(step)[1] for step in near(layers)]
    scouts = [along_y(step)[1] for step in beyond(columns)]
    scouts += [along_z(step)[1] for step in beyond(layers)]
    def greet(some):
        for friend in some:
            pl.semaphore_signal(barrier, inc=1, device_id=friend, device_id_type=MESH)

    greet(friends[:2])

    for copy in edges + inner + small:
        copy.start()
    greet(friends[2:])

    s, t = iotas()
    flip = (s + t == 127).astype(F32).astype(BF16)

    def gates(i):
        lanes = lanes_of(i)
        q, k, v, c = (ref[:, lanes].astype(F32) for ref in (q_ref, k_ref, v_ref, c_ref))
        return q, k, v, c, (k * v).astype(BF16), (c * q).astype(BF16)

    for copy in edges:
        copy.wait()

    @pl.loop(0, tiles)
    def _(i):
        lanes = lanes_of(i)
        g_edge[i] = (c_ref[low, lanes].astype(F32) * q_ref[low, lanes].astype(F32)).astype(BF16)
        u_edge[i] = (k_ref[high, lanes].astype(F32) * v_ref[high, lanes].astype(F32)).astype(BF16)

    pl.semaphore_wait(barrier, len(friends))
    sent = []

    def remote(source, target, send, receive, to):
        return pltpu.make_async_remote_copy(
            src_ref=source, dst_ref=target, send_sem=send, recv_sem=receive,
            device_id=to, device_id_type=MESH,
        )

    def u_copy(i):
        return remote(u_edge.at[i], u_halo.at[i], us.at[i], ur.at[i], right)

    def g_copy(i):
        return remote(g_edge.at[i], g_halo.at[i], gs.at[i], gr.at[i], left)

    def send(*args):
        descriptor = remote(*args)
        descriptor.start()
        sent.append(descriptor)

    @pl.loop(0, tiles)
    def _(i):
        g_copy(i).start()

    @pl.loop(0, tiles)
    def _(i):
        u_copy(i).start()

    for scout in scouts:
        pl.semaphore_signal(ready_sem, inc=1, device_id=scout, device_id_type=MESH)

    for copy in inner:
        copy.wait()

    @pl.loop(0, tiles, unroll=2)
    def _(i):
        q, k, v, c, u, g = gates(i)
        u_turned[i, :, 128:384] = u.T
        g_turned[i, :, 0:256] = g.T
        u_flip[i, 0:128] = dot(flip, u[0:128]).astype(BF16)
        u_flip[i, 128:256] = dot(flip, u[128:256]).astype(BF16)
        bias_part[pl.ds(i, 1)] = jnp.sum(u.astype(F32) * g.astype(F32), axis=0, keepdims=True)

    for copy in small:
        copy.wait()
    first_row = shard * 256
    rows = [starts_ref[pl.ds(jnp.minimum(2 * shard + b, 2 * count - 1), 1), :] - first_row for b in range(3)]
    rows[2] = rows[2] + jnp.where(shard == count - 1, 256 * count, 0)
    start = [jnp.broadcast_to(row, (128, 128)) for row in rows]
    lower = (s <= t).astype(F32)
    turned = 127 - s
    above = turned <= t
    for b in range(3):
        pair_ref[2 * b] = ((1.0 - lower) * (s + 128 * (b - 1) >= start[b]).astype(F32)).astype(BF16)
        if b < 2:
            pair_ref[2 * b + 1] = (lower * (s + 128 * b >= start[b]).astype(F32)).astype(BF16)
            limit = jnp.where(above, start[b], start[b + 1])
            lag_ref[b] = (turned + 128 * b >= limit).astype(F32)

    owner = lax.shift_right_logical(t, 4)
    none = jnp.zeros((128, 128), BF16)

    def fold(lags):
        lags = pltpu.roll(lags, 1, 1, stride=1, stride_axis=0)
        return jnp.sum(lags, axis=0, keepdims=True)

    def part_rows(i):
        return part.at[i // XS, lax.rem(i, XS)]

    def lags(i, n, b):
        mine = jnp.where(owner == n, u_flip[i, 128 * b : 128 * b + 128], none)
        products = dot(mine, g_turned[i, :, 128 * b : 128 * b + 256])
        return jnp.where(above, products[:, :128], products[:, 128:]) * lag_ref[b]

    def own_lags(i):
        for n in range(8):
            acc[i, n] = lags(i, n, 0)

    def halo_lags(i):
        for n in range(8):
            both = pltpu.roll(acc[i, n] + lags(i, n, 1), 1, 1, stride=1, stride_axis=0)
            part[i // XS, lax.rem(i, XS), n : n + 1] = jnp.sum(both, axis=0, keepdims=True)

    send(bias_part, bias_x.at[0], bc_s, bc_r, other)

    @pl.loop(0, tiles, unroll=2)
    def _(i):
        own_lags(i)

    if scouts:
        pl.semaphore_wait(ready_sem, len(scouts))
    remote(bias_part, bias_x.at[0], bc_s, bc_r, other).wait_recv()
    bias_x[1 + x] = bias_part[...] + bias_x[0]
    for step in range(1, XS):
        _, to = along_x(step)
        send(bias_x.at[1 + x], bias_x.at[1 + x], bx_s.at[step], bx_r.at[x], to)

    @pl.loop(0, tiles // 2)
    def _(j):
        for i in range(2):
            g_copy(2 * j + i).wait_recv()
        for i in range(2):
            g_turned[2 * j + i, :, 256:384] = g_halo[2 * j + i].T
        for i in range(2):
            halo_lags(2 * j + i)

    send(part.at[1 - core], half_in, c_s, c_r, other)

    @pl.loop(0, tiles)
    def _(i):
        u_copy(i).wait_recv()
        u_turned[i, :, 0:128] = u_halo[i].T

    for step in range(1, XS):
        source, to = along_x(step)
        remote(bias_x.at[1 + x], bias_x.at[1 + source], bx_s.at[step], bx_r.at[source], to).wait_recv()
    bias_y[y] = bias_x[1] + bias_x[2] + bias_x[3] + bias_x[4]
    for step in range(1, columns):
        _, to = along_y(step)
        send(bias_y.at[y], bias_y.at[y], by_s.at[step], by_r.at[y], to)

    def conv(i):
        q, k, v, c, u, g = gates(i)
        taps = taps_ref[pl.ds(pl.multiple_of(i * 8, 8), 8)].astype(BF16).astype(F32)
        for n in range(8):
            span = slice(16 * n, 16 * n + 16)
            ring = pltpu.roll(
                jnp.broadcast_to(taps[n : n + 1, :], (128, 128)), 0, 1, stride=1, stride_axis=0
            ).astype(BF16)
            p0, c0, p1, c1, p2 = (ring * pair_ref[m] for m in range(5))
            u_rows, g_rows = u_turned[i, span], g_turned[i, span]
            ct_ref[span, 0:128] = dot(u_rows[:, 0:256], jnp.concatenate([p0, c0], 0))
            ct_ref[span, 128:256] = dot(u_rows[:, 128:384], jnp.concatenate([p1, c1], 0))
            bt_ref[span, 0:128] = lax.dot_general(
                g_rows[:, 0:256], jnp.concatenate([c0, p1], 1), NT, preferred_element_type=F32
            )
            bt_ref[span, 128:256] = lax.dot_general(
                g_rows[:, 128:384], jnp.concatenate([c1, p2], 1), NT, preferred_element_type=F32
            )
        skip = skip_ref[pl.ds(i, 1)]
        filtered = ct_ref[...].T + skip * u.astype(F32)
        lanes = lanes_of(i)
        o_ref[:, lanes] = (q * filtered).astype(BF16)
        gq_ref[:, lanes] = (c * filtered).astype(BF16)
        gated_grad = bt_ref[...].T + skip * g.astype(F32)
        gk_ref[:, lanes] = (gated_grad * v).astype(BF16)
        gv_ref[:, lanes] = (gated_grad * k).astype(BF16)

    remote(part.at[1 - core], half_in, c_s, c_r, other).wait_recv()
    part[core] += half_in[...]
    for step in far_first(XS):
        to_x, to = along_x(step)
        send(part.at[core, to_x], x_in.at[x], x_s.at[step], x_r.at[x], to)
    x_in[x] = part[core, x]

    pl.loop(0, tiles // 2)(conv)

    for step in range(1, XS):
        source, to = along_x(step)
        remote(x_in.at[x], x_in.at[source], x_s.at[step], x_r.at[source], to).wait_recv()
    y_in[y] = x_in[0] + x_in[1] + x_in[2] + x_in[3]
    for step in far_first(columns):
        _, to = along_y(step)
        send(y_in.at[y], y_in.at[y], y_s.at[step], y_r.at[y], to)

    pl.loop(tiles // 2, tiles)(conv)

    for step in range(1, columns):
        source, to = along_y(step)
        remote(y_in.at[y], y_in.at[source], y_s.at[step], y_r.at[source], to).wait_recv()
    total[z, core, x] = jnp.sum(y_in[...], axis=0) * filter_scale
    own = total.at[z, core, x]
    sheet = sorted(
        ((a, b) for a in range(layers) for b in range(XS) if a or b),
        key=lambda ab: -(min(ab[0], layers - ab[0]) + min(ab[1], XS - ab[1])),
    )
    for a, b in sheet:
        to = device(y, lax.rem(x + b, XS), core, lax.rem(z + a, layers))
        send(own, own, z_s.at[a, b], z_r.at[z, x], to)

    for step in range(1, columns):
        source, to = along_y(step)
        remote(bias_y.at[y], bias_y.at[source], by_s.at[step], by_r.at[source], to).wait_recv()
    bias_total[...] = jnp.sum(bias_y[...], axis=0) * bias_scale

    @pl.loop(0, tiles)
    def _(i):
        u_copy(i).wait_send()
        g_copy(i).wait_send()

    sheet_sends = sent[-len(sheet) :]
    for descriptor in sent[: -len(sheet)]:
        descriptor.wait_send()
    sent.clear()

    span = layers // 2
    for chunk in range(2):
        for a in range(chunk * span, chunk * span + span):
            for b in range(XS):
                @pl.when((a != z) | (b != x))
                def _():
                    there = total.at[a, core, b]
                    remote(there, there, z_s.at[0, 0], z_r.at[a, b], other).wait_recv()
        block = total.at[chunk * span : chunk * span + span, core]
        send(block, block, gc_s.at[chunk], gc_r.at[chunk], other)
    for descriptor in sheet_sends:
        descriptor.wait_send()
    for chunk in range(2):
        block = total.at[chunk * span : chunk * span + span, 1 - core]
        remote(block, block, gc_s.at[chunk], gc_r.at[chunk], other).wait_recv()
    for descriptor in sent:
        descriptor.wait_send()


def whole(columns, layers, scales, q, k, v, c, filters, skip, starts):
    tokens, channels = q.shape
    tiles = channels // 128
    slice_shape = (channels // 16 // (2 * XS), 128)
    dma = pltpu.SemaphoreType.DMA
    anywhere = pl.BlockSpec(memory_space=pltpu.HBM)
    vmem = pltpu.VMEM
    block = vmem((tiles, tokens, 128), BF16)
    edge = vmem((tiles, 128, 128), BF16)
    return pl.pallas_call(
        functools.partial(whole_kernel, *scales),
        in_specs=[anywhere] * 7,
        out_specs=[pl.BlockSpec(memory_space=pltpu.VMEM)] * 6,
        out_shape=[jax.ShapeDtypeStruct((tokens, channels), BF16)] * 4
        + [
            jax.ShapeDtypeStruct((layers, 2, XS, *slice_shape), F32),
            jax.ShapeDtypeStruct((tiles, 128), F32),
        ],
        scratch_shapes=[vmem((tokens, channels), BF16)] * 4
        + [vmem((channels // 16, 128), F32), vmem((tiles, 128), F32), vmem(starts.shape, jnp.int32)]
        + [edge] * 4
        + [vmem((tiles, 128, 384), BF16)] * 2
        + [block]
        + [vmem((5, 128, 128), BF16), vmem((2, 128, 128), F32)]
        + [vmem((128, 256), F32)] * 2
        + [
            vmem((tiles, 8, 128, 128), F32),
            vmem((2, XS, *slice_shape), F32), vmem((XS, *slice_shape), F32),
            vmem((XS, *slice_shape), F32), vmem((columns, *slice_shape), F32),
            vmem((tiles, 128), F32), vmem((1 + XS, tiles, 128), F32),
            vmem((columns, tiles, 128), F32),
        ]
        + [dma((8,)), dma((3,))]
        + [dma((tiles,))] * 4
        + [dma, dma, dma((XS,)), dma((XS,)), dma((columns,)), dma((columns,))]
        + [dma, dma, dma((XS,)), dma((XS,)), dma((columns,)), dma((columns,))]
        + [dma((layers, XS)), dma((layers, XS)), dma((2,)), dma((2,)), pltpu.SemaphoreType.REGULAR],
        compiler_params=pltpu.CompilerParams(
            collective_id=0, has_side_effects=True, vmem_limit_bytes=24 * 2**20
        ),
    )(*(pltpu.with_memory_space_constraint(a, pltpu.HBM) for a in (q, k, v, c, filters, skip, starts)))


def deliver_kernel(count, *refs):
    sem = refs[-1]
    copies = [
        pltpu.make_async_copy(refs[n], refs[count + n], sem.at[n]) for n in range(count)
    ]
    for copy in copies:
        copy.start()
    for copy in copies:
        copy.wait()


def deliver(*arrays):
    return pl.pallas_call(
        functools.partial(deliver_kernel, len(arrays)),
        in_specs=[pl.BlockSpec(memory_space=pltpu.VMEM)] * len(arrays),
        out_specs=[pl.BlockSpec(memory_space=pl.ANY)] * len(arrays),
        out_shape=[jax.ShapeDtypeStruct(a.shape, a.dtype) for a in arrays],
        scratch_shapes=[pltpu.SemaphoreType.DMA((len(arrays),))],
        compiler_params=pltpu.CompilerParams(vmem_limit_bytes=20 * 2**20),
    )(*arrays)


def body(q, k, v, c, filters, skip, contig_start):
    tokens, channels = q.shape
    group_total, taps = filters.shape
    count, layers = lax.axis_size("ctx"), lax.axis_size("tp")
    token_count = tokens * count
    per_group = channels * layers // group_total
    scales = 1.0 / math.sqrt(token_count * per_group), 1.0 / math.sqrt(token_count)
    results = whole(
        count // (2 * XS), layers, scales, q, k, v, c, filters,
        skip.reshape(channels // 128, 128), contig_start.reshape(token_count // 128, 128),
    )
    o, gq, gk, gv, total, bias_total = deliver(*results)
    return o, gq, gk, gv, total.reshape(group_total, taps), bias_total.reshape(channels)


def solution(mesh):
    return jax.shard_map(
        body,
        mesh=mesh,
        in_specs=(P("ctx", "tp"),) * 4 + (P(), P("tp"), P()),
        out_specs=(P("ctx", "tp"),) * 4 + (P(), P("tp")),
        check_vma=False,
    )
```
